32 devices in a mesh: tgt: 16 (over z, y, core), sup: 2 (over x).
Axes of the slice: x: 2, y: 2, z: 4, core: 2. Of those that a mesh axis runs over, the one named last changes fastest.
Arguments:
- targets: bfloat16 [3584, 12288], P('tgt', 'sup'), may hold values from -6 to 6, as said below
- support: bfloat16 [128, 12288], P('sup'), may hold values from -6 to 6, as said below
- label_weights: bfloat16 [128, 1000], P('sup'), may hold values from -0.00390625 to 0.00390625
- labels: int32 [3584], P('tgt'), may hold values from 0 to 999
- first_moment: float32 [128, 12288], P('sup', 'tgt'), may hold values from -0.6 to 0.6
- second_moment: float32 [128, 12288], P('sup', 'tgt'), may hold values from 0.001 to 0.1
Outputs:
- new_support: bfloat16 [128, 12288], P('sup')
- new_first: float32 [128, 12288], P('sup', 'tgt')
- new_second: float32 [128, 12288], P('sup', 'tgt')
The draws below stay inside these ranges and needn't reach their ends.
Inputs may be any that keep to these rules, and one draw needn't show every extreme that they name: `targets`: image pixel values. `support`: image pixel values.
All inputs are finite; a program needn't handle non-finite values.
Results may differ from the reference program's by a relative error of at most 0.0028.
Values may be sent and summed in bfloat16 or wider, within the bound.
A program may use at most 64 MiB of HBM per device.

```python
import math
import jax
import jax.numpy as jnp
from jax import lax

P_SIZE = 12288
C = 1000
DEPTH = 3
NT = 3584
NS = 128


pattern_count = 256


def image_rows(key, count_rows, salt):
    patterns = jax.random.randint(jax.random.fold_in(key, 101), (pattern_count, P_SIZE), -4, 5).astype(jnp.float32)
    mixing = jax.random.randint(jax.random.fold_in(key, salt), (count_rows, pattern_count), -3, 4).astype(jnp.float32)
    shared = jnp.dot(mixing, patterns, precision=lax.Precision.HIGHEST) / math.sqrt(pattern_count * 60.0 / 9.0 * 4.0)
    ramp = jnp.exp(jnp.linspace(math.log(0.5), math.log(1.6), P_SIZE, dtype=jnp.float32))
    rough = jax.random.uniform(jax.random.fold_in(key, 102), (P_SIZE,), jnp.float32, 0.8, 1.2)
    noise = 0.5 * jax.random.normal(jax.random.fold_in(key, salt + 1), (count_rows, P_SIZE), jnp.float32)
    images = shared + noise
    return jnp.clip(images * (ramp * rough)[None, :], -6.0, 6.0)


def draw_targets(key, part):
    return image_rows(key, NT, 7).astype(jnp.bfloat16)


def draw_support(key, part):
    return image_rows(key, NS, 17).astype(jnp.bfloat16)


def set_ends(drawn, stream_key, least, largest):
    place = [jax.random.randint(jax.random.fold_in(stream_key, axis), (), 0, length) for axis, length in enumerate(drawn.shape)]
    main_axis = drawn.shape.index(max(drawn.shape))
    next_to = place[:main_axis] + [(place[main_axis] + 1) % drawn.shape[main_axis]] + place[main_axis + 1:]
    return drawn.at[tuple(place)].set(least).at[tuple(next_to)].set(largest)


def level_of(key, dims, pieces, least, largest):
    gain = 1.0
    for position, shards_of in pieces:
        draws = jax.random.uniform(jax.random.fold_in(jax.random.fold_in(key, 6), position), (shards_of,), jnp.float32, least / len(pieces), largest / len(pieces))
        gain = gain * jnp.repeat(jnp.exp(draws), dims[position] // shards_of).reshape((-1,) + (1,) * (len(dims) - 1 - position))
    return gain


def bell_draw(own_key, extent, width, bound, pieces=(), kind=jnp.bfloat16):
    result = width * jax.random.normal(own_key, extent, jnp.float32)
    if pieces:
        result = result * level_of(own_key, extent, pieces, -0.22, 0.18)
    return jnp.clip(result, -bound, bound).astype(kind)


def setup_inputs(seed: int = 0) -> dict:
    keys = jax.random.split(jax.random.key(seed), 7)
    targets = draw_targets(jax.random.fold_in(keys[6], 71), 0)
    support = draw_support(jax.random.fold_in(keys[6], 71), 0)
    label_weights = bell_draw(keys[2], (NS, C), (16 * C * NS) ** -0.5, 0.00390625, ((0, 2),))
    labels = set_ends(jax.random.randint(keys[3], (NT,), 0, C), jax.random.fold_in(keys[3], 1), 0, C - 1).astype(jnp.int32)
    first_moment = bell_draw(keys[4], (NS, P_SIZE), 0.1, 0.6, ((0, 2), (1, 16)), jnp.float32)
    second_moment = jnp.clip(jnp.exp(math.log(0.1) - 4.6051702 * jax.random.uniform(keys[5], (NS, P_SIZE), jnp.float32) ** level_of(keys[5], (NS, P_SIZE), ((0, 2), (1, 16)), -0.2, 0.2)), 0.001, 0.1)
    return dict(targets=targets, support=support, label_weights=label_weights, labels=labels, first_moment=first_moment, second_moment=second_moment)


bias_var = 0.1
learning_rate = 0.05
first_decay = 0.9
second_decay = 0.99
first_fix = 1.0 - 0.9 ** 10
second_fix = 1.0 - 0.99 ** 10
adam_eps = 1e-08

def tangent_kernel(cross, target_diag, support_diag):
    tangent = cross
    current = cross
    left_diag = target_diag
    right_diag = support_diag
    for _ in range(DEPTH):
        product = (1.0 + 2.0 * left_diag)[:, None] * (1.0 + 2.0 * right_diag)[None, :]
        slope = 4.0 / math.pi / jnp.sqrt(product - 4.0 * current * current)
        current = 2.0 / math.pi * jnp.arcsin(2.0 * current / jnp.sqrt(product)) + bias_var
        tangent = current + slope * tangent
        left_diag = 2.0 / math.pi * jnp.arcsin(2.0 * left_diag / (1.0 + 2.0 * left_diag)) + bias_var
        right_diag = 2.0 / math.pi * jnp.arcsin(2.0 * right_diag / (1.0 + 2.0 * right_diag)) + bias_var
    return tangent

def reference(targets, support, label_weights, labels, first_moment, second_moment):
    cross = jnp.dot(targets, support.T, preferred_element_type=jnp.float32) / P_SIZE + bias_var
    target_diag = lax.optimization_barrier(jnp.sum(jnp.square(targets.astype(jnp.float32)), axis=1)) / P_SIZE + bias_var
    support_diag = lax.optimization_barrier(jnp.sum(jnp.square(support.astype(jnp.float32)), axis=1)) / P_SIZE + bias_var

    def kernel_of(cross_in, diag_in):
        return tangent_kernel(cross_in, target_diag, diag_in)
    kernel, pullback = jax.vjp(kernel_of, cross, support_diag)
    predicted = jnp.dot(kernel.astype(jnp.bfloat16), label_weights, preferred_element_type=jnp.float32)
    classes = jnp.arange(C, dtype=jnp.int32)
    onehot = (labels[:, None] == classes[None, :]).astype(jnp.float32)
    residual = (predicted - onehot).astype(jnp.bfloat16)
    loss_scale = 4.0 * P_SIZE * math.sqrt(C * NS / NT)
    kernel_grad = jnp.dot(residual, label_weights.T, preferred_element_type=jnp.float32) * loss_scale
    cross_grad, norm_grad = pullback(kernel_grad)
    cross_low = cross_grad.astype(jnp.bfloat16)
    gradient = (jnp.dot(cross_low.T, targets, preferred_element_type=jnp.float32) + 2.0 * norm_grad[:, None] * support.astype(jnp.float32)) / P_SIZE
    new_first = first_decay * first_moment + (1.0 - first_decay) * gradient
    new_second = second_decay * second_moment + (1.0 - second_decay) * gradient * gradient
    update = learning_rate * (new_first / first_fix) / (jnp.sqrt(new_second / second_fix) + adam_eps)
    new_support = (support.astype(jnp.float32) - update).astype(jnp.bfloat16)
    return (new_support, new_first, new_second)
```

```python
import functools
import math

import jax
import jax.numpy as jnp
from jax import lax
from jax.experimental import pallas as pl
from jax.experimental.pallas import tpu as pltpu
from jax.sharding import PartitionSpec as P

DEPTH = 3


bias_var = 0.1
learning_rate = 0.05
first_decay = 0.9
second_decay = 0.99
first_fix = 1.0 - 0.9**10
second_fix = 1.0 - 0.99**10
adam_eps = 1e-08


def tangent_kernel(cross, target_diag, support_diag):
    tangent = cross
    current = cross
    left_diag = target_diag
    right_diag = support_diag
    for _ in range(DEPTH):
        product = (1.0 + 2.0 * left_diag)[:, None] * (1.0 + 2.0 * right_diag)[None, :]
        slope = 4.0 / math.pi / jnp.sqrt(product - 4.0 * current * current)
        current = 2.0 / math.pi * jnp.arcsin(2.0 * current / jnp.sqrt(product)) + bias_var
        tangent = current + slope * tangent
        left_diag = 2.0 / math.pi * jnp.arcsin(2.0 * left_diag / (1.0 + 2.0 * left_diag)) + bias_var
        right_diag = (
            2.0 / math.pi * jnp.arcsin(2.0 * right_diag / (1.0 + 2.0 * right_diag)) + bias_var
        )
    return tangent


def row_squares(images):
    return jnp.sum(jnp.square(images.astype(jnp.float32)), axis=1)


def shards(targets, support, label_weights, labels, first_moment, second_moment):
    pixels = support.shape[1]
    target_count = targets.shape[0] * lax.axis_size("tgt")
    support_count = support.shape[0] * lax.axis_size("sup")
    class_count = label_weights.shape[1]
    support_diag = row_squares(support) / pixels + bias_var
    slabs = lax.all_to_all(support, "sup", split_axis=1, concat_axis=0, tiled=True)
    partial_cross = lax.dot_general(
        targets, slabs, (((1,), (1,)), ((), ())), preferred_element_type=jnp.float32
    )
    cross = (
        lax.psum_scatter(
            partial_cross.astype(jnp.bfloat16), "sup", scatter_dimension=1, tiled=True
        ).astype(jnp.float32)
        / pixels
        + bias_var
    )
    target_diag = lax.psum(row_squares(targets), "sup") / pixels + bias_var

    def kernel_of(cross_in, diag_in):
        return tangent_kernel(cross_in, target_diag, diag_in)

    kernel, pullback = jax.vjp(kernel_of, cross, support_diag)
    partial_pred = jnp.dot(
        kernel.astype(jnp.bfloat16), label_weights, preferred_element_type=jnp.float32
    )
    predicted = lax.psum(partial_pred.astype(jnp.bfloat16), "sup").astype(jnp.float32)
    classes = jnp.arange(class_count, dtype=jnp.int32)
    onehot = (labels[:, None] == classes[None, :]).astype(jnp.float32)
    residual = (predicted - onehot).astype(jnp.bfloat16)
    kernel_grad = lax.dot_general(
        residual, label_weights, (((1,), (1,)), ((), ())), preferred_element_type=jnp.float32
    )
    kernel_grad = kernel_grad * (
        4.0 * pixels * math.sqrt(class_count * support_count / target_count)
    )
    cross_grad, norm_grad = pullback(kernel_grad)
    cross_low = cross_grad.astype(jnp.bfloat16)
    all_grads = lax.all_gather(cross_low, "sup", axis=1, tiled=True)
    slab_grad = lax.dot_general(
        all_grads, targets, (((0,), (0,)), ((), ())), preferred_element_type=jnp.float32
    )
    image_grad = lax.all_to_all(
        slab_grad.astype(jnp.bfloat16), "sup", split_axis=0, concat_axis=1, tiled=True
    ).astype(slab_grad.dtype)
    gradient = (image_grad + 2.0 * norm_grad[:, None] * support.astype(jnp.float32)) / pixels
    shares = lax.psum_scatter(gradient, "tgt", scatter_dimension=1, tiled=True)
    slab_width = shares.shape[1]
    own_pixels = lax.dynamic_slice_in_dim(
        support, lax.axis_index("tgt") * slab_width, slab_width, 1
    ).astype(jnp.float32)
    new_first = first_decay * first_moment + (1.0 - first_decay) * shares
    new_second = second_decay * second_moment + (1.0 - second_decay) * shares * shares
    update = (
        learning_rate * (new_first / first_fix) / (jnp.sqrt(new_second / second_fix) + adam_eps)
    )
    new_slab = (own_pixels - update).astype(jnp.bfloat16)
    new_support = lax.all_gather(new_slab, "tgt", axis=1, tiled=True)
    return (new_support, new_first, new_second)


MESH = pl.DeviceIdType.MESH
f32 = jnp.float32
bf16 = jnp.bfloat16


@jax.custom_jvp
def arcsine(x):
    a = jnp.abs(x)
    big = a > 0.5
    z = jnp.where(big, 0.5 * (1.0 - a), a * a)
    s = jnp.where(big, jnp.sqrt(z), a)
    p = 4.2163199048e-2 * z + 2.4181311049e-2
    p = p * z + 4.5470025998e-2
    p = p * z + 7.4953002686e-2
    p = p * z + 1.6666752422e-1
    p = p * z * s + s
    r = jnp.where(big, math.pi / 2.0 - 2.0 * p, p)
    return jnp.where(x < 0.0, -r, r)


@arcsine.defjvp
def arcsine_jvp(primals, tangents):
    (x,) = primals
    (t,) = tangents
    return arcsine(x), t * lax.rsqrt(1.0 - x * x)


def tangent_tile(cross, target_diag, support_diag):
    tangent = cross
    current = cross
    left = target_diag
    right = support_diag
    for _ in range(DEPTH):
        product = (1.0 + 2.0 * left) * (1.0 + 2.0 * right)
        slope = 4.0 / math.pi * lax.rsqrt(product - 4.0 * current * current)
        current = 2.0 / math.pi * arcsine(2.0 * current * lax.rsqrt(product)) + bias_var
        tangent = current + slope * tangent
        left = 2.0 / math.pi * arcsine(2.0 * left / (1.0 + 2.0 * left)) + bias_var
        right = 2.0 / math.pi * arcsine(2.0 * right / (1.0 + 2.0 * right)) + bias_var
    return tangent


def to_row(col, offset, lanes):
    shape = (col.shape[0], lanes)
    hit = lax.broadcasted_iota(jnp.int32, shape, 1) == lax.broadcasted_iota(jnp.int32, shape, 0) + offset
    return jnp.sum(jnp.where(hit, col, 0.0), axis=0, keepdims=True)


def to_col(row, count):
    shape = (count, row.shape[1])
    hit = lax.broadcasted_iota(jnp.int32, shape, 1) == lax.broadcasted_iota(jnp.int32, shape, 0)
    return jnp.sum(jnp.where(hit, row, 0.0), axis=1, keepdims=True)


SLAB, FWD, DIAG, CROSS, WEIGHTS, LOW, NORM = 0, 4, 8, 9, 10, 11, 12
PAIR, HALF_Y, HALF_Z, LATE_Z, LATE_Y, LAST_X, LAST_Z, LAST_A = 13, 17, 19, 21, 22, 23, 24, 25
GAT = 26
MESSAGES = 45


def step_kernel(
    scale, pixels,
    t_hbm, s_hbm, w_hbm, labels_ref, m1_ref, m2_ref,
    out_hbm, n1_ref, n2_ref,
    t_v, slab, sup_v, lw, tacc, dmsg_s, dmsg_r, cacc, cmsg_s, cmsg_r, low, nmsg_s, nmsg_r,
    s1, keep, r1, s2y, s2z, r2y, r2z, s3, r3, own, s4, r4, ns,
    send_sem, recv_sem, local_sem, out_sem,
):
    tgt = lax.axis_index("tgt")
    x = lax.axis_index("sup")
    core = lax.rem(tgt, 2)
    yy = lax.rem(tgt // 2, 2)
    z0 = lax.rem(tgt // 4, 2)
    z1 = tgt // 8
    sib_t = tgt + 1 - 2 * core
    y_t = tgt + 2 - 4 * yy
    z0_t = tgt + 4 - 8 * z0
    z1_t = tgt + 8 - 16 * z1
    SIB, YP, ZP, ZF, XP, AN = (sib_t, x), (y_t, x), (z0_t, x), (z1_t, x), (tgt, 1 - x), (z1_t, 1 - x)

    images, width = n1_ref.shape
    rows, half = t_v.shape
    mine_rows = rows // 2
    lanes = slab.shape[0]

    def remote(src, dst, number, device):
        return pltpu.make_async_remote_copy(
            src_ref=src, dst_ref=dst, send_sem=send_sem.at[number], recv_sem=recv_sem.at[number],
            device_id=device, device_id_type=MESH,
        )

    started = []

    def send(src, dst, number, device):
        copy = remote(src, dst, number, device)
        copy.start()
        started.append(copy)

    def arrived(dst, number, device):
        remote(dst, dst, number, device).wait_recv()

    def aligned(value, by):
        return pl.multiple_of(value, by)

    my_row = aligned(x * images, images)
    peer_row = aligned((1 - x) * images, images)

    load_t = pltpu.make_async_copy(t_hbm, t_v, local_sem.at[0])
    load_s = pltpu.make_async_copy(s_hbm, sup_v, local_sem.at[1])
    load_o = pltpu.make_async_copy(
        s_hbm.at[:, pl.ds(aligned(x * half, width), half)], slab.at[pl.ds(my_row, images), :], local_sem.at[2]
    )
    load_w = pltpu.make_async_copy(w_hbm, lw.at[pl.ds(my_row, images), :], local_sem.at[3])
    load_t.start()
    load_s.start()
    load_o.start()
    load_w.start()

    barrier = pltpu.get_barrier_semaphore()
    for device in (SIB, YP, ZP, ZF, XP, AN):
        pl.semaphore_signal(barrier, inc=1, device_id=device, device_id_type=MESH)
    pl.semaphore_wait(barrier, 6)

    def piece(which, index):
        return aligned((which * 4 + index) * width, width)

    for p in range(4):
        send(
            s_hbm.at[:, pl.ds(aligned((1 - x) * half + (core * 4 + p) * width, width), width)],
            slab.at[pl.ds(my_row, images), pl.ds(piece(core, p), width)],
            SLAB + p, XP,
        )

    load_s.wait()

    def support_squares(i, acc):
        block = sup_v[:, pl.ds(aligned(i * width, width), width)].astype(f32)
        block = block * block
        for k in range(width // 128):
            acc = acc + block[:, k * 128 : (k + 1) * 128]
        return acc

    sacc = lax.fori_loop(0, pixels // width, support_squares, jnp.zeros((images, 128), f32))
    s_row = to_row(jnp.sum(sacc, axis=1, keepdims=True), x * images, lanes)
    load_t.wait()
    tacc[...] = jnp.zeros_like(tacc)

    def target_squares(i, carry):
        block = t_v[:, pl.ds(aligned(i * width, width), width)].astype(f32)
        block = block * block
        acc = tacc[...]
        for k in range(width // 128):
            acc = acc + block[:, k * 128 : (k + 1) * 128]
        tacc[...] = acc
        return carry

    lax.fori_loop(0, half // width, target_squares, 0)
    peer_first = aligned((1 - x) * mine_rows, mine_rows)
    my_first = aligned(x * mine_rows, mine_rows)
    peer_sq = jnp.sum(tacc[pl.ds(peer_first, mine_rows), :], axis=1, keepdims=True)
    my_sq = jnp.sum(tacc[pl.ds(my_first, mine_rows), :], axis=1, keepdims=True)
    dmsg_s[0:8, :] = jnp.broadcast_to(to_row(peer_sq, 0, lanes), (8, lanes))
    dmsg_s[8:16, :] = jnp.broadcast_to(s_row, (8, lanes))
    send(dmsg_s, dmsg_r, DIAG, XP)

    load_o.wait()
    cacc[...] = jnp.zeros_like(cacc)

    def cross_piece(column):
        cacc[...] += lax.dot_general(
            t_v[:, pl.ds(column, width)], slab[:, pl.ds(column, width)], (((1,), (1,)), ((), ())),
            preferred_element_type=f32,
        )

    for p in range(4):
        here = slab.at[pl.ds(peer_row, images), pl.ds(piece(core, p), width)]
        arrived(here, SLAB + p, XP)
        send(here, here, FWD + p, SIB)
        cross_piece(piece(core, p))
        if p > 0:
            arrived(slab.at[pl.ds(peer_row, images), pl.ds(piece(1 - core, p - 1), width)], FWD + p - 1, SIB)
            cross_piece(piece(1 - core, p - 1))
    arrived(slab.at[pl.ds(peer_row, images), pl.ds(piece(1 - core, 3), width)], FWD + 3, SIB)
    cross_piece(piece(1 - core, 3))

    cmsg_s[...] = cacc[pl.ds(peer_first, mine_rows), :].astype(bf16)
    send(cmsg_s, cmsg_r, CROSS, XP)
    send(w_hbm, lw.at[pl.ds(my_row, images), :], WEIGHTS, XP)

    arrived(dmsg_r, DIAG, XP)
    target_diag = (my_sq + to_col(dmsg_r[0:1, :], mine_rows)) / pixels + bias_var
    support_diag = (s_row + dmsg_r[8:9, :]) / pixels + bias_var
    arrived(cmsg_r, CROSS, XP)
    cross = (cacc[pl.ds(my_first, mine_rows), :] + cmsg_r[...].astype(f32)) / pixels + bias_var

    def kernel_of(cross_in, diag_in):
        return tangent_tile(cross_in, target_diag, diag_in)

    kernel, pullback = jax.vjp(kernel_of, cross, support_diag)
    load_w.wait()
    arrived(lw.at[pl.ds(peer_row, images), :], WEIGHTS, XP)
    weights = lw[...]
    predicted = jnp.dot(kernel.astype(bf16), weights, preferred_element_type=f32)
    classes = lax.broadcasted_iota(jnp.int32, predicted.shape, 1)
    onehot = (labels_ref[pl.ds(my_first, mine_rows), :] == classes).astype(f32)
    residual = (predicted - onehot).astype(bf16)
    kernel_grad = scale * lax.dot_general(
        residual, weights, (((1,), (1,)), ((), ())), preferred_element_type=f32
    )
    cross_grad, norm_grad = pullback(kernel_grad)
    mine_low = low.at[pl.ds(my_first, mine_rows), :]
    mine_low[...] = cross_grad.astype(bf16)
    nmsg_s[...] = jnp.broadcast_to(norm_grad, nmsg_s.shape)
    send(mine_low, mine_low, LOW, XP)
    send(nmsg_s, nmsg_r, NORM, XP)
    arrived(low.at[pl.ds(peer_first, mine_rows), :], LOW, XP)
    arrived(nmsg_r, NORM, XP)
    norm_col = to_col(2.0 * (norm_grad + nmsg_r[0:1, :]), lanes)
    grads = low[...]

    order = ((1, 1), (0, 1), (1, 0), (0, 0))
    chunk = 256 if width % 256 == 0 else 128

    def slab_grad(index, other, store):
        dz, dy = order[index]
        number = (z0 + dz - 2 * dz * z0) * 4 + (yy + dy - 2 * dy * yy) * 2 + (1 - core if other else core)

        def body(i, carry):
            columns = pl.ds(aligned(number * width + i * chunk, chunk), chunk)
            value = lax.dot_general(
                grads, t_v[:, columns], (((0,), (0,)), ((), ())), preferred_element_type=f32
            )
            value = value + norm_col * slab[:, columns].astype(f32)
            store(pl.ds(aligned(i * chunk, chunk), chunk), value)
            return carry

        lax.fori_loop(0, width // chunk, body, 0)

    for k in range(4):
        def store_sent(columns, value, k=k):
            s1[k, :, columns] = value.astype(bf16)

        slab_grad(k, True, store_sent)
        send(s1.at[k], r1.at[k], PAIR + k, SIB)
    for k in range(4):
        def store_kept(columns, value, k=k):
            keep[k, :, columns] = value

        slab_grad(k, False, store_kept)

    first = slice(0, images)
    second = slice(images, 2 * images)

    def pair_sum(k, part):
        return keep[k, part, :] + r1[k, part, :].astype(f32)

    arrived(r1.at[0], PAIR, SIB)
    s2y[0] = pair_sum(0, first).astype(bf16)
    send(s2y.at[0], r2y.at[0], HALF_Y, YP)
    s2z[0] = pair_sum(0, second).astype(bf16)
    send(s2z.at[0], r2z.at[0], HALF_Z, ZP)
    arrived(r1.at[1], PAIR + 1, SIB)
    s2y[1] = pair_sum(1, first).astype(bf16)
    send(s2y.at[1], r2y.at[1], HALF_Y + 1, YP)
    arrived(r1.at[2], PAIR + 2, SIB)
    s2z[1] = pair_sum(2, second).astype(bf16)
    send(s2z.at[1], r2z.at[1], HALF_Z + 1, ZP)

    arrived(r2y.at[0], HALF_Y, YP)
    s3[0] = (pair_sum(2, first) + r2y[0].astype(f32)).astype(bf16)
    send(s3.at[0], r3.at[0], LATE_Z, ZP)
    arrived(r2z.at[0], HALF_Z, ZP)
    s3[1] = (pair_sum(1, second) + r2z[0].astype(f32)).astype(bf16)
    send(s3.at[1], r3.at[1], LATE_Y, YP)
    arrived(r1.at[3], PAIR + 3, SIB)
    arrived(r2y.at[1], HALF_Y + 1, YP)
    own[0] = pair_sum(3, first) + r2y[1].astype(f32)
    arrived(r2z.at[1], HALF_Z + 1, ZP)
    own[1] = pair_sum(3, second) + r2z[1].astype(f32)
    arrived(r3.at[0], LATE_Z, ZP)
    own[0] = own[0] + r3[0].astype(f32)
    s4[0] = own[0].astype(bf16)
    arrived(r3.at[1], LATE_Y, YP)
    own[1] = own[1] + r3[1].astype(f32)
    s4[1] = own[1].astype(bf16)

    home = z1 == x
    last_x = remote(s4.at[1 - x], r4.at[0], LAST_X, XP)
    last_z = remote(s4.at[x], r4.at[1], LAST_Z, ZF)
    last_a = remote(s4.at[1 - x], r4.at[1], LAST_A, AN)

    @pl.when(home)
    def _():
        last_x.start()
        last_z.wait_recv()
        keep[0, first, :] = own[x] + r4[1].astype(f32)
        last_x.wait_send()

    @pl.when(jnp.logical_not(home))
    def _():
        last_a.start()
        last_z.start()
        last_x.wait_recv()
        last_a.wait_recv()
        keep[0, first, :] = r4[0].astype(f32) + r4[1].astype(f32)
        last_a.wait_send()
        last_z.wait_send()

    def block(ref, index, part=slice(None)):
        return ref.at[part, pl.ds(aligned(index * width, width), width)]

    gradient = keep[0, first, :] / pixels
    new_first = first_decay * m1_ref[...] + (1.0 - first_decay) * gradient
    new_second = second_decay * m2_ref[...] + (1.0 - second_decay) * gradient * gradient
    update = learning_rate * (new_first / first_fix) / (jnp.sqrt(new_second / second_fix) + adam_eps)
    mine = pl.ds(aligned(tgt * width, width), width)
    ns[:, mine] = (sup_v[:, mine].astype(f32) - update).astype(bf16)
    n1_ref[...] = new_first
    n2_ref[...] = new_second

    low_half, high_half = slice(0, images // 2), slice(images // 2, images)
    z1y_t = y_t + z1_t - tgt
    z1z0_t = z0_t + z1_t - tgt
    d_t = y_t + z0_t - tgt
    z1d_t = d_t + z1_t - tgt
    swap = sib_t - tgt

    def pass_on(index, number, device, part=slice(None)):
        send(block(ns, index, part), block(ns, index, part), number, device)

    def came(index, number, device, part=slice(None)):
        arrived(block(ns, index, part), number, device)

    pass_on(tgt, GAT, ZF)
    pass_on(tgt, GAT + 1, YP)
    pass_on(tgt, GAT + 2, ZP)
    pass_on(tgt, GAT + 3, SIB)
    came(z1_t, GAT, ZF)
    pass_on(z1_t, GAT + 4, YP)
    pass_on(z1_t, GAT + 5, ZP)
    pass_on(z1_t, GAT + 6, SIB)
    came(y_t, GAT + 1, YP)
    pass_on(y_t, GAT + 7, ZP, high_half)
    pass_on(y_t, GAT + 8, SIB)
    came(z0_t, GAT + 2, ZP)
    pass_on(z0_t, GAT + 9, YP, low_half)
    pass_on(z0_t, GAT + 10, SIB)
    came(z1y_t, GAT + 4, YP)
    pass_on(z1y_t, GAT + 11, ZP, high_half)
    pass_on(z1y_t, GAT + 12, SIB)
    came(z1z0_t, GAT + 5, ZP)
    pass_on(z1z0_t, GAT + 13, YP, low_half)
    pass_on(z1z0_t, GAT + 14, SIB)
    came(d_t, GAT + 7, ZP, high_half)
    pass_on(d_t, GAT + 15, SIB, high_half)
    came(d_t, GAT + 9, YP, low_half)
    pass_on(d_t, GAT + 16, SIB, low_half)
    came(z1d_t, GAT + 11, ZP, high_half)
    pass_on(z1d_t, GAT + 17, SIB, high_half)
    came(z1d_t, GAT + 13, YP, low_half)
    pass_on(z1d_t, GAT + 18, SIB, low_half)

    came(tgt + swap, GAT + 3, SIB)
    came(z1_t + swap, GAT + 6, SIB)
    came(y_t + swap, GAT + 8, SIB)
    came(z0_t + swap, GAT + 10, SIB)
    came(z1y_t + swap, GAT + 12, SIB)
    came(z1z0_t + swap, GAT + 14, SIB)
    came(d_t + swap, GAT + 15, SIB, high_half)
    came(d_t + swap, GAT + 16, SIB, low_half)
    came(z1d_t + swap, GAT + 17, SIB, high_half)
    came(z1d_t + swap, GAT + 18, SIB, low_half)
    store = pltpu.make_async_copy(ns, out_hbm, out_sem)
    store.start()
    for copy in started:
        copy.wait_send()
    store.wait()


def fused(targets, support, label_weights, labels, first_moment, second_moment):
    rows, half = targets.shape
    images, pixels = support.shape
    width = first_moment.shape[1]
    classes = label_weights.shape[1]
    target_count = rows * lax.axis_size("tgt")
    support_count = images * lax.axis_size("sup")
    scale = 4.0 * pixels * math.sqrt(classes * support_count / target_count)
    everyone, part = 2 * images, rows // 2
    hbm = pl.BlockSpec(memory_space=pl.ANY)
    vmem = pl.BlockSpec(memory_space=pltpu.VMEM)
    return pl.pallas_call(
        functools.partial(step_kernel, scale, pixels),
        out_shape=(
            jax.ShapeDtypeStruct(support.shape, bf16),
            jax.ShapeDtypeStruct(first_moment.shape, f32),
            jax.ShapeDtypeStruct(first_moment.shape, f32),
        ),
        in_specs=[hbm, hbm, hbm, vmem, vmem, vmem],
        out_specs=(hbm, vmem, vmem),
        scratch_shapes=[
            pltpu.VMEM((rows, half), bf16),
            pltpu.VMEM((everyone, half), bf16),
            pltpu.VMEM((images, pixels), bf16),
            pltpu.VMEM((everyone, classes), bf16),
            pltpu.VMEM((rows, 128), f32),
            pltpu.VMEM((16, everyone), f32),
            pltpu.VMEM((16, everyone), f32),
            pltpu.VMEM((rows, everyone), f32),
            pltpu.VMEM((part, everyone), bf16),
            pltpu.VMEM((part, everyone), bf16),
            pltpu.VMEM((rows, everyone), bf16),
            pltpu.VMEM((8, everyone), f32),
            pltpu.VMEM((8, everyone), f32),
            pltpu.VMEM((4, everyone, width), bf16),
            pltpu.VMEM((4, everyone, width), f32),
            pltpu.VMEM((4, everyone, width), bf16),
            pltpu.VMEM((2, images, width), bf16),
            pltpu.VMEM((2, images, width), bf16),
            pltpu.VMEM((2, images, width), bf16),
            pltpu.VMEM((2, images, width), bf16),
            pltpu.VMEM((2, images, width), bf16),
            pltpu.VMEM((2, images, width), bf16),
            pltpu.VMEM((2, images, width), f32),
            pltpu.VMEM((2, images, width), bf16),
            pltpu.VMEM((2, images, width), bf16),
            pltpu.VMEM((images, pixels), bf16),
            pltpu.SemaphoreType.DMA((MESSAGES,)),
            pltpu.SemaphoreType.DMA((MESSAGES,)),
            pltpu.SemaphoreType.DMA((4,)),
            pltpu.SemaphoreType.DMA,
        ],
        compiler_params=pltpu.CompilerParams(
            collective_id=0, has_side_effects=True, vmem_limit_bytes=48 * 1024 * 1024
        ),
    )(targets, support, label_weights, labels[:, None], first_moment, second_moment)


def pick(mesh):
    groups, shares = mesh.shape["sup"], mesh.shape["tgt"]

    def run(targets, support, label_weights, labels, first_moment, second_moment):
        width = first_moment.shape[1]
        fits = groups == 2 and shares == 16 and width % 128 == 0
        fits = fits and targets.shape[0] % 32 == 0 and groups * support.shape[0] == 128
        body = fused if fits else shards
        return body(targets, support, label_weights, labels, first_moment, second_moment)

    return run


def solution(mesh):
    return jax.shard_map(
        pick(mesh),
        mesh=mesh,
        in_specs=(
            P("tgt", "sup"),
            P("sup", None),
            P("sup", None),
            P("tgt"),
            P("sup", "tgt"),
            P("sup", "tgt"),
        ),
        out_specs=(P("sup", None), P("sup", "tgt"), P("sup", "tgt")),
        check_vma=False,
    )
```

```python
import functools
import math

import jax
import jax.numpy as jnp
from jax import lax
from jax.experimental import pallas as pl
from jax.experimental.pallas import tpu as pltpu
from jax.sharding import PartitionSpec as P

DEPTH = 3


bias_var = 0.1
learning_rate = 0.05
first_decay = 0.9
second_decay = 0.99
first_fix = 1.0 - 0.9**10
second_fix = 1.0 - 0.99**10
adam_eps = 1e-08


def tangent_kernel(cross, target_diag, support_diag):
    tangent = cross
    current = cross
    left_diag = target_diag
    right_diag = support_diag
    for _ in range(DEPTH):
        product = (1.0 + 2.0 * left_diag)[:, None] * (1.0 + 2.0 * right_diag)[None, :]
        slope = 4.0 / math.pi / jnp.sqrt(product - 4.0 * current * current)
        current = 2.0 / math.pi * jnp.arcsin(2.0 * current / jnp.sqrt(product)) + bias_var
        tangent = current + slope * tangent
        left_diag = 2.0 / math.pi * jnp.arcsin(2.0 * left_diag / (1.0 + 2.0 * left_diag)) + bias_var
        right_diag = (
            2.0 / math.pi * jnp.arcsin(2.0 * right_diag / (1.0 + 2.0 * right_diag)) + bias_var
        )
    return tangent


def row_squares(images):
    return jnp.sum(jnp.square(images.astype(jnp.float32)), axis=1)


def shards(targets, support, label_weights, labels, first_moment, second_moment):
    pixels = support.shape[1]
    target_count = targets.shape[0] * lax.axis_size("tgt")
    support_count = support.shape[0] * lax.axis_size("sup")
    class_count = label_weights.shape[1]
    support_diag = row_squares(support) / pixels + bias_var
    slabs = lax.all_to_all(support, "sup", split_axis=1, concat_axis=0, tiled=True)
    partial_cross = lax.dot_general(
        targets, slabs, (((1,), (1,)), ((), ())), preferred_element_type=jnp.float32
    )
    cross = (
        lax.psum_scatter(
            partial_cross.astype(jnp.bfloat16), "sup", scatter_dimension=1, tiled=True
        ).astype(jnp.float32)
        / pixels
        + bias_var
    )
    target_diag = lax.psum(row_squares(targets), "sup") / pixels + bias_var

    def kernel_of(cross_in, diag_in):
        return tangent_kernel(cross_in, target_diag, diag_in)

    kernel, pullback = jax.vjp(kernel_of, cross, support_diag)
    partial_pred = jnp.dot(
        kernel.astype(jnp.bfloat16), label_weights, preferred_element_type=jnp.float32
    )
    predicted = lax.psum(partial_pred.astype(jnp.bfloat16), "sup").astype(jnp.float32)
    classes = jnp.arange(class_count, dtype=jnp.int32)
    onehot = (labels[:, None] == classes[None, :]).astype(jnp.float32)
    residual = (predicted - onehot).astype(jnp.bfloat16)
    kernel_grad = lax.dot_general(
        residual, label_weights, (((1,), (1,)), ((), ())), preferred_element_type=jnp.float32
    )
    kernel_grad = kernel_grad * (
        4.0 * pixels * math.sqrt(class_count * support_count / target_count)
    )
    cross_grad, norm_grad = pullback(kernel_grad)
    cross_low = cross_grad.astype(jnp.bfloat16)
    all_grads = lax.all_gather(cross_low, "sup", axis=1, tiled=True)
    slab_grad = lax.dot_general(
        all_grads, targets, (((0,), (0,)), ((), ())), preferred_element_type=jnp.float32
    )
    image_grad = lax.all_to_all(
        slab_grad.astype(jnp.bfloat16), "sup", split_axis=0, concat_axis=1, tiled=True
    ).astype(slab_grad.dtype)
    gradient = (image_grad + 2.0 * norm_grad[:, None] * support.astype(jnp.float32)) / pixels
    shares = lax.psum_scatter(gradient, "tgt", scatter_dimension=1, tiled=True)
    slab_width = shares.shape[1]
    own_pixels = lax.dynamic_slice_in_dim(
        support, lax.axis_index("tgt") * slab_width, slab_width, 1
    ).astype(jnp.float32)
    new_first = first_decay * first_moment + (1.0 - first_decay) * shares
    new_second = second_decay * second_moment + (1.0 - second_decay) * shares * shares
    update = (
        learning_rate * (new_first / first_fix) / (jnp.sqrt(new_second / second_fix) + adam_eps)
    )
    new_slab = (own_pixels - update).astype(jnp.bfloat16)
    new_support = lax.all_gather(new_slab, "tgt", axis=1, tiled=True)
    return (new_support, new_first, new_second)


MESH = pl.DeviceIdType.MESH
f32 = jnp.float32
bf16 = jnp.bfloat16


@jax.custom_jvp
def arcsine(x):
    a = jnp.abs(x)
    big = a > 0.5
    z = jnp.where(big, 0.5 * (1.0 - a), a * a)
    s = jnp.where(big, jnp.sqrt(z), a)
    p = 4.2163199048e-2 * z + 2.4181311049e-2
    p = p * z + 4.5470025998e-2
    p = p * z + 7.4953002686e-2
    p = p * z + 1.6666752422e-1
    p = p * z * s + s
    r = jnp.where(big, math.pi / 2.0 - 2.0 * p, p)
    return jnp.where(x < 0.0, -r, r)


@arcsine.defjvp
def arcsine_jvp(primals, tangents):
    (x,) = primals
    (t,) = tangents
    return arcsine(x), t * lax.rsqrt(1.0 - x * x)


def tangent_tile(cross, target_diag, support_diag):
    tangent = cross
    current = cross
    left = target_diag
    right = support_diag
    for _ in range(DEPTH):
        product = (1.0 + 2.0 * left) * (1.0 + 2.0 * right)
        slope = 4.0 / math.pi * lax.rsqrt(product - 4.0 * current * current)
        current = 2.0 / math.pi * arcsine(2.0 * current * lax.rsqrt(product)) + bias_var
        tangent = current + slope * tangent
        left = 2.0 / math.pi * arcsine(2.0 * left / (1.0 + 2.0 * left)) + bias_var
        right = 2.0 / math.pi * arcsine(2.0 * right / (1.0 + 2.0 * right)) + bias_var
    return tangent


def to_row(col, offset, lanes):
    shape = (col.shape[0], lanes)
    hit = lax.broadcasted_iota(jnp.int32, shape, 1) == lax.broadcasted_iota(jnp.int32, shape, 0) + offset
    return jnp.sum(jnp.where(hit, col, 0.0), axis=0, keepdims=True)


def to_col(row, count, offset=0):
    shape = (count, row.shape[1])
    hit = lax.broadcasted_iota(jnp.int32, shape, 1) == lax.broadcasted_iota(jnp.int32, shape, 0) + offset
    return jnp.sum(jnp.where(hit, row, 0.0), axis=1, keepdims=True)


SLAB, FWD, DIAG, CROSS, WEIGHTS, LOW, NORM = 0, 4, 8, 9, 10, 11, 12
PAIR, HALF_Y, HALF_Z, LATE_Z, LATE_Y, LAST_X, LAST_Z, LAST_A = 13, 17, 19, 21, 22, 23, 24, 25
GAT = 26
MESSAGES = 51


def step_kernel(
    scale, pixels,
    t_hbm, s_hbm, w_hbm, labels_hbm, m1_hbm, m2_hbm,
    out_hbm, n1_ref, n2_ref,
    t_v, slab, sup_v, lw, tacc, dmsg_s, dmsg_r, cacc, cmsg_s, cmsg_r, low, nmsg_s, nmsg_r,
    s1, keep, r1, s2y, s2z, r2y, r2z, s3, r3, own, s4, r4, ns, labels_ref, m1_ref, m2_ref,
    send_sem, recv_sem, local_sem, out_sem,
):
    tgt = lax.axis_index("tgt")
    x = lax.axis_index("sup")
    core = lax.rem(tgt, 2)
    yy = lax.rem(tgt // 2, 2)
    z0 = lax.rem(tgt // 4, 2)
    z1 = tgt // 8
    sib_t = tgt + 1 - 2 * core
    y_t = tgt + 2 - 4 * yy
    z0_t = tgt + 4 - 8 * z0
    z1_t = tgt + 8 - 16 * z1
    SIB, YP, ZP, ZF, XP, AN = (sib_t, x), (y_t, x), (z0_t, x), (z1_t, x), (tgt, 1 - x), (z1_t, 1 - x)

    images, width = n1_ref.shape
    rows, half = t_v.shape
    mine_rows = rows // 2
    lanes = slab.shape[0]

    def remote(src, dst, number, device):
        return pltpu.make_async_remote_copy(
            src_ref=src, dst_ref=dst, send_sem=send_sem.at[number], recv_sem=recv_sem.at[number],
            device_id=device, device_id_type=MESH,
        )

    started = []

    def send(src, dst, number, device):
        copy = remote(src, dst, number, device)
        copy.start()
        started.append(copy)

    def arrived(dst, number, device):
        remote(dst, dst, number, device).wait_recv()

    def aligned(value, by):
        return pl.multiple_of(value, by)

    my_row = aligned(x * images, images)
    peer_row = aligned((1 - x) * images, images)

    load_t = pltpu.make_async_copy(t_hbm, t_v, local_sem.at[0])
    load_s = pltpu.make_async_copy(s_hbm, sup_v, local_sem.at[1])
    load_o = pltpu.make_async_copy(
        s_hbm.at[:, pl.ds(aligned(x * half, width), half)], slab.at[pl.ds(my_row, images), :], local_sem.at[2]
    )
    load_w = pltpu.make_async_copy(w_hbm, lw.at[pl.ds(my_row, images), :], local_sem.at[3])
    load_t.start()
    load_s.start()
    load_o.start()
    load_w.start()
    load_l = pltpu.make_async_copy(labels_hbm, labels_ref, local_sem.at[4])
    load_1 = pltpu.make_async_copy(m1_hbm, m1_ref, local_sem.at[5])
    load_2 = pltpu.make_async_copy(m2_hbm, m2_ref, local_sem.at[6])
    load_l.start()
    load_1.start()
    load_2.start()

    barrier = pltpu.get_barrier_semaphore()
    for device in (SIB, YP, ZP, ZF, XP, AN):
        pl.semaphore_signal(barrier, inc=1, device_id=device, device_id_type=MESH)
    pl.semaphore_wait(barrier, 6)

    def piece(which, index):
        return aligned((which * 4 + index) * width, width)

    seat = 2 * yy + z0
    turn = (seat, 3 - seat, seat + 2 - 4 * yy, seat + 1 - 2 * z0)
    source = (XP, XP, YP, ZP)
    for p in range(2):
        send(
            s_hbm.at[:, pl.ds(aligned((1 - x) * half + (core * 4 + turn[p]) * width, width), width)],
            slab.at[pl.ds(my_row, images), pl.ds(aligned((core * 4 + turn[p]) * width, width), width)],
            SLAB + p, XP,
        )
    send(w_hbm, lw.at[pl.ds(my_row, images), :], WEIGHTS, XP)

    load_s.wait()

    def support_squares(i, acc):
        block = sup_v[:, pl.ds(aligned(i * width, width), width)].astype(f32)
        block = block * block
        for k in range(width // 128):
            acc = acc + block[:, k * 128 : (k + 1) * 128]
        return acc

    sacc = lax.fori_loop(0, pixels // width, support_squares, jnp.zeros((images, 128), f32))
    s_row = to_row(jnp.sum(sacc, axis=1, keepdims=True), x * images, lanes)
    load_t.wait()
    tacc[...] = jnp.zeros_like(tacc)

    def target_squares(i, carry):
        block = t_v[:, pl.ds(aligned(i * width, width), width)].astype(f32)
        block = block * block
        acc = tacc[...]
        for k in range(width // 128):
            acc = acc + block[:, k * 128 : (k + 1) * 128]
        tacc[...] = acc
        return carry

    lax.fori_loop(0, half // width, target_squares, 0)
    peer_first = aligned((1 - x) * mine_rows, mine_rows)
    my_first = aligned(x * mine_rows, mine_rows)
    peer_sq = jnp.sum(tacc[pl.ds(peer_first, mine_rows), :], axis=1, keepdims=True)
    my_sq = jnp.sum(tacc[pl.ds(my_first, mine_rows), :], axis=1, keepdims=True)
    load_l.wait()
    label_col = to_col(labels_ref[...].astype(f32), mine_rows, x * mine_rows)
    dmsg_s[0:8, :] = jnp.broadcast_to(to_row(peer_sq, 0, lanes), (8, lanes))
    dmsg_s[8:16, :] = jnp.broadcast_to(s_row, (8, lanes))
    send(dmsg_s, dmsg_r, DIAG, XP)

    load_o.wait()
    cacc[...] = jnp.zeros_like(cacc)

    def cross_piece(column):
        cacc[...] += lax.dot_general(
            t_v[:, pl.ds(column, width)], slab[:, pl.ds(column, width)], (((1,), (1,)), ((), ())),
            preferred_element_type=f32,
        )

    for p in range(4):
        here = slab.at[pl.ds(peer_row, images), pl.ds(piece(core, turn[p]), width)]
        arrived(here, SLAB + p, source[p])
        if p == 0:
            send(here, here, SLAB + 2, YP)
            send(here, here, SLAB + 3, ZP)
        send(here, here, FWD + p, SIB)
        cross_piece(piece(core, turn[p]))
        if p > 0:
            there = piece(1 - core, turn[p - 1])
            arrived(slab.at[pl.ds(peer_row, images), pl.ds(there, width)], FWD + p - 1, SIB)
            cross_piece(there)
    there = piece(1 - core, turn[3])
    arrived(slab.at[pl.ds(peer_row, images), pl.ds(there, width)], FWD + 3, SIB)
    cross_piece(there)

    cmsg_s[...] = cacc[pl.ds(peer_first, mine_rows), :].astype(bf16)
    send(cmsg_s, cmsg_r, CROSS, XP)

    arrived(dmsg_r, DIAG, XP)
    target_diag = (my_sq + to_col(dmsg_r[0:1, :], mine_rows)) / pixels + bias_var
    support_diag = (s_row + dmsg_r[8:9, :]) / pixels + bias_var
    arrived(cmsg_r, CROSS, XP)
    cross = (cacc[pl.ds(my_first, mine_rows), :] + cmsg_r[...].astype(f32)) / pixels + bias_var

    def kernel_of(cross_in, diag_in):
        return tangent_tile(cross_in, target_diag, diag_in)

    kernel, pullback = jax.vjp(kernel_of, cross, support_diag)
    load_w.wait()
    arrived(lw.at[pl.ds(peer_row, images), :], WEIGHTS, XP)
    weights = lw[...]
    predicted = jnp.dot(kernel.astype(bf16), weights, preferred_element_type=f32)
    classes = lax.broadcasted_iota(jnp.int32, predicted.shape, 1)
    onehot = (label_col == classes.astype(f32)).astype(f32)
    residual = (predicted - onehot).astype(bf16)
    kernel_grad = scale * lax.dot_general(
        residual, weights, (((1,), (1,)), ((), ())), preferred_element_type=f32
    )
    cross_grad, norm_grad = pullback(kernel_grad)
    mine_low = low.at[pl.ds(my_first, mine_rows), :]
    mine_low[...] = cross_grad.astype(bf16)
    nmsg_s[...] = jnp.broadcast_to(norm_grad, nmsg_s.shape)
    send(mine_low, mine_low, LOW, XP)
    send(nmsg_s, nmsg_r, NORM, XP)
    arrived(low.at[pl.ds(peer_first, mine_rows), :], LOW, XP)
    arrived(nmsg_r, NORM, XP)
    norm_col = to_col(2.0 * (norm_grad + nmsg_r[0:1, :]), lanes)
    grads = low[...]

    order = ((1, 1), (0, 1), (1, 0), (0, 0))
    chunk = 256 if width % 256 == 0 else 128

    def slab_grad(index, other, store):
        dz, dy = order[index]
        number = (z0 + dz - 2 * dz * z0) * 4 + (yy + dy - 2 * dy * yy) * 2 + (1 - core if other else core)

        def body(i, carry):
            columns = pl.ds(aligned(number * width + i * chunk, chunk), chunk)
            value = lax.dot_general(
                grads, t_v[:, columns], (((0,), (0,)), ((), ())), preferred_element_type=f32
            )
            value = value + norm_col * slab[:, columns].astype(f32)
            store(pl.ds(aligned(i * chunk, chunk), chunk), value)
            return carry

        lax.fori_loop(0, width // chunk, body, 0)

    first = slice(0, images)
    second = slice(images, 2 * images)

    def pair_sum(k, part):
        return keep[k, part, :] + r1[k, part, :].astype(f32)

    def give(k):
        def store(columns, value):
            s1[k, :, columns] = value.astype(bf16)

        slab_grad(k, True, store)
        send(s1.at[k], r1.at[k], PAIR + k, SIB)

    def hold(k):
        def store(columns, value):
            keep[k, :, columns] = value

        slab_grad(k, False, store)

    give(0)
    give(1)
    hold(0)
    arrived(r1.at[0], PAIR, SIB)
    s2y[0] = pair_sum(0, first).astype(bf16)
    send(s2y.at[0], r2y.at[0], HALF_Y, YP)
    s2z[0] = pair_sum(0, second).astype(bf16)
    send(s2z.at[0], r2z.at[0], HALF_Z, ZP)
    give(2)
    hold(1)
    arrived(r1.at[1], PAIR + 1, SIB)
    s2y[1] = pair_sum(1, first).astype(bf16)
    send(s2y.at[1], r2y.at[1], HALF_Y + 1, YP)
    hold(2)
    arrived(r1.at[2], PAIR + 2, SIB)
    s2z[1] = pair_sum(2, second).astype(bf16)
    send(s2z.at[1], r2z.at[1], HALF_Z + 1, ZP)
    give(3)
    hold(3)

    arrived(r2y.at[0], HALF_Y, YP)
    s3[0] = (pair_sum(2, first) + r2y[0].astype(f32)).astype(bf16)
    send(s3.at[0], r3.at[0], LATE_Z, ZP)
    arrived(r2z.at[0], HALF_Z, ZP)
    s3[1] = (pair_sum(1, second) + r2z[0].astype(f32)).astype(bf16)
    send(s3.at[1], r3.at[1], LATE_Y, YP)
    arrived(r1.at[3], PAIR + 3, SIB)
    arrived(r2y.at[1], HALF_Y + 1, YP)
    own[0] = pair_sum(3, first) + r2y[1].astype(f32)
    arrived(r2z.at[1], HALF_Z + 1, ZP)
    own[1] = pair_sum(3, second) + r2z[1].astype(f32)
    arrived(r3.at[0], LATE_Z, ZP)
    own[0] = own[0] + r3[0].astype(f32)
    s4[0] = own[0].astype(bf16)
    arrived(r3.at[1], LATE_Y, YP)
    own[1] = own[1] + r3[1].astype(f32)
    s4[1] = own[1].astype(bf16)

    home = z1 == x
    last_x = remote(s4.at[1 - x], r4.at[0], LAST_X, XP)
    last_z = remote(s4.at[x], r4.at[1], LAST_Z, ZF)
    last_a = remote(s4.at[1 - x], r4.at[1], LAST_A, AN)

    @pl.when(home)
    def _():
        last_x.start()
        last_z.wait_recv()
        keep[0, first, :] = own[x] + r4[1].astype(f32)
        last_x.wait_send()

    @pl.when(jnp.logical_not(home))
    def _():
        last_a.start()
        last_z.start()
        last_x.wait_recv()
        last_a.wait_recv()
        keep[0, first, :] = r4[0].astype(f32) + r4[1].astype(f32)
        last_a.wait_send()
        last_z.wait_send()

    def block(ref, index, part=slice(None)):
        return ref.at[part, pl.ds(aligned(index * width, width), width)]

    load_1.wait()
    load_2.wait()
    gradient = keep[0, first, :] / pixels
    new_first = first_decay * m1_ref[...] + (1.0 - first_decay) * gradient
    new_second = second_decay * m2_ref[...] + (1.0 - second_decay) * gradient * gradient
    update = learning_rate * (new_first / first_fix) / (jnp.sqrt(new_second / second_fix) + adam_eps)
    mine = pl.ds(aligned(tgt * width, width), width)
    ns[:, mine] = (sup_v[:, mine].astype(f32) - update).astype(bf16)
    n1_ref[...] = new_first
    n2_ref[...] = new_second

    low_half, high_half = slice(0, images // 2), slice(images // 2, images)
    z1y_t = y_t + z1_t - tgt
    z1z0_t = z0_t + z1_t - tgt
    d_t = y_t + z0_t - tgt
    z1d_t = d_t + z1_t - tgt
    swap = sib_t - tgt

    def pass_on(index, number, device, part=slice(None)):
        send(block(ns, index, part), block(ns, index, part), number, device)

    def came(index, number, device, part=slice(None)):
        arrived(block(ns, index, part), number, device)

    halves = (low_half, high_half)
    pass_on(tgt, GAT, ZF, low_half)
    pass_on(tgt, GAT + 1, ZF, high_half)
    pass_on(tgt, GAT + 2, YP)
    pass_on(tgt, GAT + 3, ZP)
    pass_on(tgt, GAT + 4, SIB)
    came(y_t, GAT + 2, YP)
    pass_on(y_t, GAT + 5, ZP, high_half)
    pass_on(y_t, GAT + 6, SIB)
    came(z0_t, GAT + 3, ZP)
    pass_on(z0_t, GAT + 7, YP, low_half)
    pass_on(z0_t, GAT + 8, SIB)
    for h in (0, 1):
        came(z1_t, GAT + h, ZF, halves[h])
        pass_on(z1_t, GAT + 9 + h, YP, halves[h])
        pass_on(z1_t, GAT + 11 + h, ZP, halves[h])
        pass_on(z1_t, GAT + 13 + h, SIB, halves[h])
    came(d_t, GAT + 5, ZP, high_half)
    pass_on(d_t, GAT + 15, SIB, high_half)
    came(d_t, GAT + 7, YP, low_half)
    pass_on(d_t, GAT + 16, SIB, low_half)
    for h in (0, 1):
        came(z1z0_t, GAT + 11 + h, ZP, halves[h])
        if h == 0:
            pass_on(z1z0_t, GAT + 17, YP, low_half)
        pass_on(z1z0_t, GAT + 18 + h, SIB, halves[h])
        came(z1y_t, GAT + 9 + h, YP, halves[h])
        if h == 1:
            pass_on(z1y_t, GAT + 20, ZP, high_half)
        pass_on(z1y_t, GAT + 21 + h, SIB, halves[h])
    came(z1d_t, GAT + 17, YP, low_half)
    pass_on(z1d_t, GAT + 23, SIB, low_half)
    came(z1d_t, GAT + 20, ZP, high_half)
    pass_on(z1d_t, GAT + 24, SIB, high_half)

    came(tgt + swap, GAT + 4, SIB)
    came(y_t + swap, GAT + 6, SIB)
    came(z0_t + swap, GAT + 8, SIB)
    came(d_t + swap, GAT + 15, SIB, high_half)
    came(d_t + swap, GAT + 16, SIB, low_half)
    for h in (0, 1):
        came(z1_t + swap, GAT + 13 + h, SIB, halves[h])
        came(z1z0_t + swap, GAT + 18 + h, SIB, halves[h])
        came(z1y_t + swap, GAT + 21 + h, SIB, halves[h])
    came(z1d_t + swap, GAT + 23, SIB, low_half)
    came(z1d_t + swap, GAT + 24, SIB, high_half)
    store = pltpu.make_async_copy(ns, out_hbm, out_sem)
    store.start()
    for copy in started:
        copy.wait_send()
    store.wait()


def fused(targets, support, label_weights, labels, first_moment, second_moment):
    rows, half = targets.shape
    images, pixels = support.shape
    width = first_moment.shape[1]
    classes = label_weights.shape[1]
    target_count = rows * lax.axis_size("tgt")
    support_count = images * lax.axis_size("sup")
    scale = 4.0 * pixels * math.sqrt(classes * support_count / target_count)
    everyone, part = 2 * images, rows // 2
    hbm = pl.BlockSpec(memory_space=pltpu.HBM)
    vmem = pl.BlockSpec(memory_space=pltpu.VMEM)
    return pl.pallas_call(
        functools.partial(step_kernel, scale, pixels),
        out_shape=(
            jax.ShapeDtypeStruct(support.shape, bf16),
            jax.ShapeDtypeStruct(first_moment.shape, f32),
            jax.ShapeDtypeStruct(first_moment.shape, f32),
        ),
        in_specs=[hbm] * 6,
        out_specs=(pl.BlockSpec(memory_space=pl.ANY), vmem, vmem),
        scratch_shapes=[
            pltpu.VMEM((rows, half), bf16),
            pltpu.VMEM((everyone, half), bf16),
            pltpu.VMEM((images, pixels), bf16),
            pltpu.VMEM((everyone, classes), bf16),
            pltpu.VMEM((rows, 128), f32),
            pltpu.VMEM((16, everyone), f32),
            pltpu.VMEM((16, everyone), f32),
            pltpu.VMEM((rows, everyone), f32),
            pltpu.VMEM((part, everyone), bf16),
            pltpu.VMEM((part, everyone), bf16),
            pltpu.VMEM((rows, everyone), bf16),
            pltpu.VMEM((8, everyone), f32),
            pltpu.VMEM((8, everyone), f32),
            pltpu.VMEM((4, everyone, width), bf16),
            pltpu.VMEM((4, everyone, width), f32),
            pltpu.VMEM((4, everyone, width), bf16),
            pltpu.VMEM((2, images, width), bf16),
            pltpu.VMEM((2, images, width), bf16),
            pltpu.VMEM((2, images, width), bf16),
            pltpu.VMEM((2, images, width), bf16),
            pltpu.VMEM((2, images, width), bf16),
            pltpu.VMEM((2, images, width), bf16),
            pltpu.VMEM((2, images, width), f32),
            pltpu.VMEM((2, images, width), bf16),
            pltpu.VMEM((2, images, width), bf16),
            pltpu.VMEM((images, pixels), bf16),
            pltpu.VMEM((1, rows), jnp.int32),
            pltpu.VMEM((images, width), f32),
            pltpu.VMEM((images, width), f32),
            pltpu.SemaphoreType.DMA((MESSAGES,)),
            pltpu.SemaphoreType.DMA((MESSAGES,)),
            pltpu.SemaphoreType.DMA((7,)),
            pltpu.SemaphoreType.DMA,
        ],
        compiler_params=pltpu.CompilerParams(
            collective_id=0, has_side_effects=True, vmem_limit_bytes=60000000
        ),
    )(targets, support, label_weights, labels[None, :], first_moment, second_moment)


def pick(mesh):
    groups, shares = mesh.shape["sup"], mesh.shape["tgt"]

    def run(targets, support, label_weights, labels, first_moment, second_moment):
        width = first_moment.shape[1]
        fits = groups == 2 and shares == 16 and width % 128 == 0
        fits = fits and targets.shape[0] % 32 == 0 and groups * support.shape[0] == 128
        body = fused if fits else shards
        return body(targets, support, label_weights, labels, first_moment, second_moment)

    return run


def solution(mesh):
    return jax.shard_map(
        pick(mesh),
        mesh=mesh,
        in_specs=(
            P("tgt", "sup"),
            P("sup", None),
            P("sup", None),
            P("tgt"),
            P("sup", "tgt"),
            P("sup", "tgt"),
        ),
        out_specs=(P("sup", None), P("sup", "tgt"), P("sup", "tgt")),
        check_vma=False,
    )
```

```python
import functools
import math

import jax
import jax.numpy as jnp
from jax import lax
from jax.experimental import pallas as pl
from jax.experimental.pallas import tpu as pltpu
from jax.sharding import PartitionSpec as P

DEPTH = 3


bias_var = 0.1
learning_rate = 0.05
first_decay = 0.9
second_decay = 0.99
first_fix = 1.0 - 0.9**10
second_fix = 1.0 - 0.99**10
adam_eps = 1e-08


def tangent_kernel(cross, target_diag, support_diag):
    tangent = cross
    current = cross
    left_diag = target_diag
    right_diag = support_diag
    for _ in range(DEPTH):
        product = (1.0 + 2.0 * left_diag)[:, None] * (1.0 + 2.0 * right_diag)[None, :]
        slope = 4.0 / math.pi / jnp.sqrt(product - 4.0 * current * current)
        current = 2.0 / math.pi * jnp.arcsin(2.0 * current / jnp.sqrt(product)) + bias_var
        tangent = current + slope * tangent
        left_diag = 2.0 / math.pi * jnp.arcsin(2.0 * left_diag / (1.0 + 2.0 * left_diag)) + bias_var
        right_diag = (
            2.0 / math.pi * jnp.arcsin(2.0 * right_diag / (1.0 + 2.0 * right_diag)) + bias_var
        )
    return tangent


def row_squares(images):
    return jnp.sum(jnp.square(images.astype(jnp.float32)), axis=1)


def shards(targets, support, label_weights, labels, first_moment, second_moment):
    pixels = support.shape[1]
    target_count = targets.shape[0] * lax.axis_size("tgt")
    support_count = support.shape[0] * lax.axis_size("sup")
    class_count = label_weights.shape[1]
    support_diag = row_squares(support) / pixels + bias_var
    slabs = lax.all_to_all(support, "sup", split_axis=1, concat_axis=0, tiled=True)
    partial_cross = lax.dot_general(
        targets, slabs, (((1,), (1,)), ((), ())), preferred_element_type=jnp.float32
    )
    cross = (
        lax.psum_scatter(
            partial_cross.astype(jnp.bfloat16), "sup", scatter_dimension=1, tiled=True
        ).astype(jnp.float32)
        / pixels
        + bias_var
    )
    target_diag = lax.psum(row_squares(targets), "sup") / pixels + bias_var

    def kernel_of(cross_in, diag_in):
        return tangent_kernel(cross_in, target_diag, diag_in)

    kernel, pullback = jax.vjp(kernel_of, cross, support_diag)
    partial_pred = jnp.dot(
        kernel.astype(jnp.bfloat16), label_weights, preferred_element_type=jnp.float32
    )
    predicted = lax.psum(partial_pred.astype(jnp.bfloat16), "sup").astype(jnp.float32)
    classes = jnp.arange(class_count, dtype=jnp.int32)
    onehot = (labels[:, None] == classes[None, :]).astype(jnp.float32)
    residual = (predicted - onehot).astype(jnp.bfloat16)
    kernel_grad = lax.dot_general(
        residual, label_weights, (((1,), (1,)), ((), ())), preferred_element_type=jnp.float32
    )
    kernel_grad = kernel_grad * (
        4.0 * pixels * math.sqrt(class_count * support_count / target_count)
    )
    cross_grad, norm_grad = pullback(kernel_grad)
    cross_low = cross_grad.astype(jnp.bfloat16)
    all_grads = lax.all_gather(cross_low, "sup", axis=1, tiled=True)
    slab_grad = lax.dot_general(
        all_grads, targets, (((0,), (0,)), ((), ())), preferred_element_type=jnp.float32
    )
    image_grad = lax.all_to_all(
        slab_grad.astype(jnp.bfloat16), "sup", split_axis=0, concat_axis=1, tiled=True
    ).astype(slab_grad.dtype)
    gradient = (image_grad + 2.0 * norm_grad[:, None] * support.astype(jnp.float32)) / pixels
    shares = lax.psum_scatter(gradient, "tgt", scatter_dimension=1, tiled=True)
    slab_width = shares.shape[1]
    own_pixels = lax.dynamic_slice_in_dim(
        support, lax.axis_index("tgt") * slab_width, slab_width, 1
    ).astype(jnp.float32)
    new_first = first_decay * first_moment + (1.0 - first_decay) * shares
    new_second = second_decay * second_moment + (1.0 - second_decay) * shares * shares
    update = (
        learning_rate * (new_first / first_fix) / (jnp.sqrt(new_second / second_fix) + adam_eps)
    )
    new_slab = (own_pixels - update).astype(jnp.bfloat16)
    new_support = lax.all_gather(new_slab, "tgt", axis=1, tiled=True)
    return (new_support, new_first, new_second)


MESH = pl.DeviceIdType.MESH
f32 = jnp.float32
bf16 = jnp.bfloat16


@jax.custom_jvp
def arcsine(x):
    a = jnp.abs(x)
    big = a > 0.5
    z = jnp.where(big, 0.5 * (1.0 - a), a * a)
    s = jnp.where(big, jnp.sqrt(z), a)
    p = 4.2163199048e-2 * z + 2.4181311049e-2
    p = p * z + 4.5470025998e-2
    p = p * z + 7.4953002686e-2
    p = p * z + 1.6666752422e-1
    p = p * z * s + s
    r = jnp.where(big, math.pi / 2.0 - 2.0 * p, p)
    return jnp.where(x < 0.0, -r, r)


@arcsine.defjvp
def arcsine_jvp(primals, tangents):
    (x,) = primals
    (t,) = tangents
    return arcsine(x), t * lax.rsqrt(1.0 - x * x)


def tangent_tile(cross, target_diag, support_diag):
    tangent = cross
    current = cross
    left = target_diag
    right = support_diag
    for _ in range(DEPTH):
        product = (1.0 + 2.0 * left) * (1.0 + 2.0 * right)
        slope = 4.0 / math.pi * lax.rsqrt(product - 4.0 * current * current)
        current = 2.0 / math.pi * arcsine(2.0 * current * lax.rsqrt(product)) + bias_var
        tangent = current + slope * tangent
        left = 2.0 / math.pi * arcsine(2.0 * left / (1.0 + 2.0 * left)) + bias_var
        right = 2.0 / math.pi * arcsine(2.0 * right / (1.0 + 2.0 * right)) + bias_var
    return tangent


def to_row(col, offset, lanes):
    shape = (col.shape[0], lanes)
    hit = lax.broadcasted_iota(jnp.int32, shape, 1) == lax.broadcasted_iota(jnp.int32, shape, 0) + offset
    return jnp.sum(jnp.where(hit, col, 0.0), axis=0, keepdims=True)


def to_col(row, count, offset=0):
    shape = (count, row.shape[1])
    hit = lax.broadcasted_iota(jnp.int32, shape, 1) == lax.broadcasted_iota(jnp.int32, shape, 0) + offset
    return jnp.sum(jnp.where(hit, row, 0.0), axis=1, keepdims=True)


SLAB, FWD, DIAG, CROSS, WEIGHTS, LOW, NORM = 0, 4, 8, 9, 10, 11, 12
PAIR, HALF_Y, HALF_Z, LATE_Z, LATE_Y, LAST_X, LAST_Z, LAST_A = 13, 17, 19, 21, 22, 23, 24, 25
GAT = 26
MESSAGES = 51


def step_kernel(
    scale, pixels,
    t_hbm, s_hbm, w_hbm, labels_hbm, m1_hbm, m2_hbm,
    out_hbm, n1_ref, n2_ref,
    t_v, slab, sup_v, lw, tacc, dmsg_s, dmsg_r, cacc, cmsg_s, cmsg_r, low, nmsg_s, nmsg_r,
    s1, keep, r1, s2y, s2z, r2y, r2z, s3, r3, own, s4, r4, ns, labels_ref, m1_ref, m2_ref,
    send_sem, recv_sem, local_sem, out_sem,
):
    tgt = lax.axis_index("tgt")
    x = lax.axis_index("sup")
    core = lax.rem(tgt, 2)
    yy = lax.rem(tgt // 2, 2)
    z0 = lax.rem(tgt // 4, 2)
    z1 = tgt // 8
    sib_t = tgt + 1 - 2 * core
    y_t = tgt + 2 - 4 * yy
    z0_t = tgt + 4 - 8 * z0
    z1_t = tgt + 8 - 16 * z1
    SIB, YP, ZP, ZF, XP, AN = (sib_t, x), (y_t, x), (z0_t, x), (z1_t, x), (tgt, 1 - x), (z1_t, 1 - x)

    images, width = n1_ref.shape
    rows, half = t_v.shape
    mine_rows = rows // 2
    lanes = slab.shape[0]

    def remote(src, dst, number, device):
        return pltpu.make_async_remote_copy(
            src_ref=src, dst_ref=dst, send_sem=send_sem.at[number], recv_sem=recv_sem.at[number],
            device_id=device, device_id_type=MESH,
        )

    started = []

    def send(src, dst, number, device):
        copy = remote(src, dst, number, device)
        copy.start()
        started.append(copy)

    def arrived(dst, number, device):
        remote(dst, dst, number, device).wait_recv()

    def aligned(value, by):
        return pl.multiple_of(value, by)

    my_row = aligned(x * images, images)
    peer_row = aligned((1 - x) * images, images)

    load_t = pltpu.make_async_copy(t_hbm, t_v, local_sem.at[0])
    load_s = pltpu.make_async_copy(s_hbm, sup_v, local_sem.at[1])
    load_o = pltpu.make_async_copy(
        s_hbm.at[:, pl.ds(aligned(x * half, width), half)], slab.at[pl.ds(my_row, images), :], local_sem.at[2]
    )
    load_w = pltpu.make_async_copy(w_hbm, lw.at[pl.ds(my_row, images), :], local_sem.at[3])
    load_t.start()
    load_s.start()
    load_o.start()
    load_w.start()
    load_l = pltpu.make_async_copy(labels_hbm, labels_ref, local_sem.at[4])
    load_1 = pltpu.make_async_copy(m1_hbm, m1_ref, local_sem.at[5])
    load_2 = pltpu.make_async_copy(m2_hbm, m2_ref, local_sem.at[6])
    load_l.start()
    load_1.start()
    load_2.start()

    barrier = pltpu.get_barrier_semaphore()
    for device in (SIB, YP, ZP, ZF, XP, AN):
        pl.semaphore_signal(barrier, inc=1, device_id=device, device_id_type=MESH)
    load_s.wait()

    def support_squares(i, acc):
        block = sup_v[:, pl.ds(aligned(i * width, width), width)].astype(f32)
        block = block * block
        for k in range(width // 128):
            acc = acc + block[:, k * 128 : (k + 1) * 128]
        return acc

    sacc = lax.fori_loop(0, pixels // width, support_squares, jnp.zeros((images, 128), f32))
    s_row = to_row(jnp.sum(sacc, axis=1, keepdims=True), x * images, lanes)
    pl.semaphore_wait(barrier, 6)

    def piece(which, index):
        return aligned((which * 4 + index) * width, width)

    seat = 2 * yy + z0
    turn = (seat, 3 - seat, seat + 2 - 4 * yy, seat + 1 - 2 * z0)
    source = (XP, XP, YP, ZP)
    for p in range(2):
        send(
            s_hbm.at[:, pl.ds(aligned((1 - x) * half + (core * 4 + turn[p]) * width, width), width)],
            slab.at[pl.ds(my_row, images), pl.ds(aligned((core * 4 + turn[p]) * width, width), width)],
            SLAB + p, XP,
        )
    send(w_hbm, lw.at[pl.ds(my_row, images), :], WEIGHTS, XP)

    def target_sums():
        load_t.wait()
        tacc[...] = jnp.zeros_like(tacc)

        def target_squares(i, carry):
            block = t_v[:, pl.ds(aligned(i * width, width), width)].astype(f32)
            block = block * block
            acc = tacc[...]
            for k in range(width // 128):
                acc = acc + block[:, k * 128 : (k + 1) * 128]
            tacc[...] = acc
            return carry

        lax.fori_loop(0, half // width, target_squares, 0)
        peer_first = aligned((1 - x) * mine_rows, mine_rows)
        my_first = aligned(x * mine_rows, mine_rows)
        peer_sq = jnp.sum(tacc[pl.ds(peer_first, mine_rows), :], axis=1, keepdims=True)
        my_sq = jnp.sum(tacc[pl.ds(my_first, mine_rows), :], axis=1, keepdims=True)
        load_l.wait()
        label_col = to_col(labels_ref[...].astype(f32), mine_rows, x * mine_rows)
        dmsg_s[0:8, :] = jnp.broadcast_to(to_row(peer_sq, 0, lanes), (8, lanes))
        dmsg_s[8:16, :] = jnp.broadcast_to(s_row, (8, lanes))
        send(dmsg_s, dmsg_r, DIAG, XP)
        return my_sq, my_first, peer_first, label_col

    load_o.wait()
    cacc[...] = jnp.zeros_like(cacc)

    def cross_piece(column):
        cacc[...] += lax.dot_general(
            t_v[:, pl.ds(column, width)], slab[:, pl.ds(column, width)], (((1,), (1,)), ((), ())),
            preferred_element_type=f32,
        )

    for p in range(4):
        here = slab.at[pl.ds(peer_row, images), pl.ds(piece(core, turn[p]), width)]
        arrived(here, SLAB + p, source[p])
        if p == 0:
            send(here, here, SLAB + 2, YP)
            send(here, here, SLAB + 3, ZP)
        send(here, here, FWD + p, SIB)
        if p == 0:
            my_sq, my_first, peer_first, label_col = target_sums()
        cross_piece(piece(core, turn[p]))
        if p > 0:
            there = piece(1 - core, turn[p - 1])
            arrived(slab.at[pl.ds(peer_row, images), pl.ds(there, width)], FWD + p - 1, SIB)
            cross_piece(there)
    there = piece(1 - core, turn[3])
    arrived(slab.at[pl.ds(peer_row, images), pl.ds(there, width)], FWD + 3, SIB)
    cross_piece(there)

    cmsg_s[...] = cacc[pl.ds(peer_first, mine_rows), :].astype(bf16)
    send(cmsg_s, cmsg_r, CROSS, XP)

    arrived(dmsg_r, DIAG, XP)
    target_diag = (my_sq + to_col(dmsg_r[0:1, :], mine_rows)) / pixels + bias_var
    support_diag = (s_row + dmsg_r[8:9, :]) / pixels + bias_var
    arrived(cmsg_r, CROSS, XP)
    cross = (cacc[pl.ds(my_first, mine_rows), :] + cmsg_r[...].astype(f32)) / pixels + bias_var

    def kernel_of(cross_in, diag_in):
        return tangent_tile(cross_in, target_diag, diag_in)

    kernel, pullback = jax.vjp(kernel_of, cross, support_diag)
    load_w.wait()
    arrived(lw.at[pl.ds(peer_row, images), :], WEIGHTS, XP)
    weights = lw[...]
    predicted = jnp.dot(kernel.astype(bf16), weights, preferred_element_type=f32)
    classes = lax.broadcasted_iota(jnp.int32, predicted.shape, 1)
    onehot = (label_col == classes.astype(f32)).astype(f32)
    residual = (predicted - onehot).astype(bf16)
    kernel_grad = scale * lax.dot_general(
        residual, weights, (((1,), (1,)), ((), ())), preferred_element_type=f32
    )
    cross_grad, norm_grad = pullback(kernel_grad)
    mine_low = low.at[pl.ds(my_first, mine_rows), :]
    mine_low[...] = cross_grad.astype(bf16)
    nmsg_s[...] = jnp.broadcast_to(norm_grad, nmsg_s.shape)
    send(mine_low, mine_low, LOW, XP)
    send(nmsg_s, nmsg_r, NORM, XP)
    arrived(low.at[pl.ds(peer_first, mine_rows), :], LOW, XP)
    arrived(nmsg_r, NORM, XP)
    norm_col = to_col(2.0 * (norm_grad + nmsg_r[0:1, :]), lanes)
    grads = low[...]

    order = ((1, 1), (0, 1), (1, 0), (0, 0))
    chunk = 256 if width % 256 == 0 else 128

    def slab_grad(index, other, store):
        dz, dy = order[index]
        number = (z0 + dz - 2 * dz * z0) * 4 + (yy + dy - 2 * dy * yy) * 2 + (1 - core if other else core)

        def body(i, carry):
            columns = pl.ds(aligned(number * width + i * chunk, chunk), chunk)
            value = lax.dot_general(
                grads, t_v[:, columns], (((0,), (0,)), ((), ())), preferred_element_type=f32
            )
            value = value + norm_col * slab[:, columns].astype(f32)
            store(pl.ds(aligned(i * chunk, chunk), chunk), value)
            return carry

        lax.fori_loop(0, width // chunk, body, 0)

    first = slice(0, images)
    second = slice(images, 2 * images)

    def pair_sum(k, part):
        return keep[k, part, :] + r1[k, part, :].astype(f32)

    def give(k):
        def store(columns, value):
            s1[k, :, columns] = value.astype(bf16)

        slab_grad(k, True, store)
        send(s1.at[k], r1.at[k], PAIR + k, SIB)

    def hold(k):
        def store(columns, value):
            keep[k, :, columns] = value

        slab_grad(k, False, store)

    give(0)
    give(1)
    hold(0)
    arrived(r1.at[0], PAIR, SIB)
    s2y[0] = pair_sum(0, first).astype(bf16)
    send(s2y.at[0], r2y.at[0], HALF_Y, YP)
    s2z[0] = pair_sum(0, second).astype(bf16)
    send(s2z.at[0], r2z.at[0], HALF_Z, ZP)
    give(2)
    hold(1)
    arrived(r1.at[1], PAIR + 1, SIB)
    s2y[1] = pair_sum(1, first).astype(bf16)
    send(s2y.at[1], r2y.at[1], HALF_Y + 1, YP)
    hold(2)
    arrived(r1.at[2], PAIR + 2, SIB)
    s2z[1] = pair_sum(2, second).astype(bf16)
    send(s2z.at[1], r2z.at[1], HALF_Z + 1, ZP)
    give(3)
    hold(3)

    arrived(r2y.at[0], HALF_Y, YP)
    s3[0] = (pair_sum(2, first) + r2y[0].astype(f32)).astype(bf16)
    send(s3.at[0], r3.at[0], LATE_Z, ZP)
    arrived(r2z.at[0], HALF_Z, ZP)
    s3[1] = (pair_sum(1, second) + r2z[0].astype(f32)).astype(bf16)
    send(s3.at[1], r3.at[1], LATE_Y, YP)
    arrived(r1.at[3], PAIR + 3, SIB)
    arrived(r2y.at[1], HALF_Y + 1, YP)
    own[0] = pair_sum(3, first) + r2y[1].astype(f32)
    arrived(r2z.at[1], HALF_Z + 1, ZP)
    own[1] = pair_sum(3, second) + r2z[1].astype(f32)
    arrived(r3.at[0], LATE_Z, ZP)
    own[0] = own[0] + r3[0].astype(f32)
    s4[0] = own[0].astype(bf16)
    arrived(r3.at[1], LATE_Y, YP)
    own[1] = own[1] + r3[1].astype(f32)
    s4[1] = own[1].astype(bf16)

    home = z1 == x
    last_x = remote(s4.at[1 - x], r4.at[0], LAST_X, XP)
    last_z = remote(s4.at[x], r4.at[1], LAST_Z, ZF)
    last_a = remote(s4.at[1 - x], r4.at[1], LAST_A, AN)

    @pl.when(home)
    def _():
        last_x.start()
        last_z.wait_recv()
        keep[0, first, :] = own[x] + r4[1].astype(f32)
        last_x.wait_send()

    @pl.when(jnp.logical_not(home))
    def _():
        last_a.start()
        last_z.start()
        last_x.wait_recv()
        last_a.wait_recv()
        keep[0, first, :] = r4[0].astype(f32) + r4[1].astype(f32)
        last_a.wait_send()
        last_z.wait_send()

    def block(ref, index, part=slice(None)):
        return ref.at[part, pl.ds(aligned(index * width, width), width)]

    load_1.wait()
    load_2.wait()
    gradient = keep[0, first, :] / pixels
    new_first = first_decay * m1_ref[...] + (1.0 - first_decay) * gradient
    new_second = second_decay * m2_ref[...] + (1.0 - second_decay) * gradient * gradient
    update = learning_rate * (new_first / first_fix) / (jnp.sqrt(new_second / second_fix) + adam_eps)
    mine = pl.ds(aligned(tgt * width, width), width)
    ns[:, mine] = (sup_v[:, mine].astype(f32) - update).astype(bf16)
    n1_ref[...] = new_first
    n2_ref[...] = new_second

    low_half, high_half = slice(0, images // 2), slice(images // 2, images)
    z1y_t = y_t + z1_t - tgt
    z1z0_t = z0_t + z1_t - tgt
    d_t = y_t + z0_t - tgt
    z1d_t = d_t + z1_t - tgt
    swap = sib_t - tgt

    def pass_on(index, number, device, part=slice(None)):
        send(block(ns, index, part), block(ns, index, part), number, device)

    def came(index, number, device, part=slice(None)):
        arrived(block(ns, index, part), number, device)

    halves = (low_half, high_half)
    pass_on(tgt, GAT, ZF, low_half)
    pass_on(tgt, GAT + 1, ZF, high_half)
    pass_on(tgt, GAT + 2, YP)
    pass_on(tgt, GAT + 3, ZP)
    pass_on(tgt, GAT + 4, SIB)
    came(y_t, GAT + 2, YP)
    pass_on(y_t, GAT + 5, ZP, high_half)
    pass_on(y_t, GAT + 6, SIB)
    came(z0_t, GAT + 3, ZP)
    pass_on(z0_t, GAT + 7, YP, low_half)
    pass_on(z0_t, GAT + 8, SIB)
    for h in (0, 1):
        came(z1_t, GAT + h, ZF, halves[h])
        pass_on(z1_t, GAT + 9 + h, YP, halves[h])
        pass_on(z1_t, GAT + 11 + h, ZP, halves[h])
        pass_on(z1_t, GAT + 13 + h, SIB, halves[h])
    came(d_t, GAT + 5, ZP, high_half)
    pass_on(d_t, GAT + 15, SIB, high_half)
    came(d_t, GAT + 7, YP, low_half)
    pass_on(d_t, GAT + 16, SIB, low_half)
    for h in (0, 1):
        came(z1z0_t, GAT + 11 + h, ZP, halves[h])
        if h == 0:
            pass_on(z1z0_t, GAT + 17, YP, low_half)
        pass_on(z1z0_t, GAT + 18 + h, SIB, halves[h])
        came(z1y_t, GAT + 9 + h, YP, halves[h])
        if h == 1:
            pass_on(z1y_t, GAT + 20, ZP, high_half)
        pass_on(z1y_t, GAT + 21 + h, SIB, halves[h])
    came(z1d_t, GAT + 17, YP, low_half)
    pass_on(z1d_t, GAT + 23, SIB, low_half)
    came(z1d_t, GAT + 20, ZP, high_half)
    pass_on(z1d_t, GAT + 24, SIB, high_half)

    came(tgt + swap, GAT + 4, SIB)
    came(y_t + swap, GAT + 6, SIB)
    came(z0_t + swap, GAT + 8, SIB)
    came(d_t + swap, GAT + 15, SIB, high_half)
    came(d_t + swap, GAT + 16, SIB, low_half)
    for h in (0, 1):
        came(z1_t + swap, GAT + 13 + h, SIB, halves[h])
        came(z1z0_t + swap, GAT + 18 + h, SIB, halves[h])
        came(z1y_t + swap, GAT + 21 + h, SIB, halves[h])
    came(z1d_t + swap, GAT + 23, SIB, low_half)
    came(z1d_t + swap, GAT + 24, SIB, high_half)
    store = pltpu.make_async_copy(ns, out_hbm, out_sem)
    store.start()
    for copy in started:
        copy.wait_send()
    store.wait()


def fused(targets, support, label_weights, labels, first_moment, second_moment):
    rows, half = targets.shape
    images, pixels = support.shape
    width = first_moment.shape[1]
    classes = label_weights.shape[1]
    target_count = rows * lax.axis_size("tgt")
    support_count = images * lax.axis_size("sup")
    scale = 4.0 * pixels * math.sqrt(classes * support_count / target_count)
    everyone, part = 2 * images, rows // 2
    hbm = pl.BlockSpec(memory_space=pltpu.HBM)
    vmem = pl.BlockSpec(memory_space=pltpu.VMEM)
    return pl.pallas_call(
        functools.partial(step_kernel, scale, pixels),
        out_shape=(
            jax.ShapeDtypeStruct(support.shape, bf16),
            jax.ShapeDtypeStruct(first_moment.shape, f32),
            jax.ShapeDtypeStruct(first_moment.shape, f32),
        ),
        in_specs=[hbm] * 6,
        out_specs=(pl.BlockSpec(memory_space=pl.ANY), vmem, vmem),
        scratch_shapes=[
            pltpu.VMEM((rows, half), bf16),
            pltpu.VMEM((everyone, half), bf16),
            pltpu.VMEM((images, pixels), bf16),
            pltpu.VMEM((everyone, classes), bf16),
            pltpu.VMEM((rows, 128), f32),
            pltpu.VMEM((16, everyone), f32),
            pltpu.VMEM((16, everyone), f32),
            pltpu.VMEM((rows, everyone), f32),
            pltpu.VMEM((part, everyone), bf16),
            pltpu.VMEM((part, everyone), bf16),
            pltpu.VMEM((rows, everyone), bf16),
            pltpu.VMEM((8, everyone), f32),
            pltpu.VMEM((8, everyone), f32),
            pltpu.VMEM((4, everyone, width), bf16),
            pltpu.VMEM((4, everyone, width), f32),
            pltpu.VMEM((4, everyone, width), bf16),
            pltpu.VMEM((2, images, width), bf16),
            pltpu.VMEM((2, images, width), bf16),
            pltpu.VMEM((2, images, width), bf16),
            pltpu.VMEM((2, images, width), bf16),
            pltpu.VMEM((2, images, width), bf16),
            pltpu.VMEM((2, images, width), bf16),
            pltpu.VMEM((2, images, width), f32),
            pltpu.VMEM((2, images, width), bf16),
            pltpu.VMEM((2, images, width), bf16),
            pltpu.VMEM((images, pixels), bf16),
            pltpu.VMEM((1, rows), jnp.int32),
            pltpu.VMEM((images, width), f32),
            pltpu.VMEM((images, width), f32),
            pltpu.SemaphoreType.DMA((MESSAGES,)),
            pltpu.SemaphoreType.DMA((MESSAGES,)),
            pltpu.SemaphoreType.DMA((7,)),
            pltpu.SemaphoreType.DMA,
        ],
        compiler_params=pltpu.CompilerParams(
            collective_id=0, has_side_effects=True, vmem_limit_bytes=60000000
        ),
    )(targets, support, label_weights, labels[None, :], first_moment, second_moment)


def pick(mesh):
    groups, shares = mesh.shape["sup"], mesh.shape["tgt"]

    def run(targets, support, label_weights, labels, first_moment, second_moment):
        width = first_moment.shape[1]
        fits = groups == 2 and shares == 16 and width % 128 == 0
        fits = fits and targets.shape[0] % 32 == 0 and groups * support.shape[0] == 128
        body = fused if fits else shards
        return body(targets, support, label_weights, labels, first_moment, second_moment)

    return run


def solution(mesh):
    return jax.shard_map(
        pick(mesh),
        mesh=mesh,
        in_specs=(
            P("tgt", "sup"),
            P("sup", None),
            P("sup", None),
            P("tgt"),
            P("sup", "tgt"),
            P("sup", "tgt"),
        ),
        out_specs=(P("sup", None), P("sup", "tgt"), P("sup", "tgt")),
        check_vma=False,
    )
```
